32 devices in a mesh: dp: 16 (over z, y, core), tensor: 2 (over x).
Axes of the slice: x: 2, y: 2, z: 4, core: 2. Of those that a mesh axis runs over, the one named last changes fastest.
Arguments:
- tokens: bfloat16 [4096, 1024], P(('dp', 'tensor')), may hold values from -24 to 24, as said below
- segment_ids: int32 [16, 256], P('dp'), may hold values from 0 to 3, never falling along the last dimension, each value on 1 to 128 neighbouring positions
- norm1_gain: float32 [1024], replicated, may hold values from 0.5 to 1.5
- in_proj: bfloat16 [1024, 3, 1024], P('dp', None, 'tensor'), may hold values from -0.1875 to 0.1875
- conv_weight: float32 [3, 1024], replicated, may hold values from -3 to 3
- out_proj: bfloat16 [1024, 1024], P('dp', 'tensor'), may hold values from -0.1875 to 0.1875
- norm2_gain: float32 [1024], replicated, may hold values from 0.5 to 1.5
- gate_up: bfloat16 [1024, 2, 4608], P('dp', None, 'tensor'), may hold values from -0.1875 to 0.1875
- down_proj: bfloat16 [1024, 4608], P('dp', 'tensor'), may hold values from -0.1875 to 0.1875
- cotangent: bfloat16 [4096, 1024], P(('dp', 'tensor')), may hold values from -6 to 6
Outputs:
- block_out: float32 [4096, 1024], P(('dp', 'tensor'))
- grad_tokens: float32 [4096, 1024], P(('dp', 'tensor'))
- grad_norm1: float32 [1024], replicated
- grad_in_proj: float32 [1024, 3, 1024], P('dp', None, 'tensor')
- grad_conv: float32 [3, 1024], replicated
- grad_out_proj: float32 [1024, 1024], P('dp', 'tensor')
- grad_norm2: float32 [1024], replicated
- grad_gate_up: float32 [1024, 2, 4608], P('dp', None, 'tensor')
- grad_down: float32 [1024, 4608], P('dp', 'tensor')
The draws below stay inside these ranges and needn't reach their ends.
Inputs may be any that keep to these rules, and one draw needn't show every extreme that they name: `segment_ids`: along each row the document numbers never fall; each document spans 1 to 128 tokens and one spans exactly 128. `tokens`: real values.
All inputs are finite; a program needn't handle non-finite values.
Results may differ from the reference program's by a relative error of at most 0.009.
Values may be sent and summed in bfloat16 or wider, within the bound.
A program may use at most 128 MiB of HBM per device.

```python
import math
import jax
import jax.numpy as jnp
import numpy as np
from jax import lax

D = 1024
FF = 4608
TOK_DEV = 256
SEGS = 4
MOST_DOC = 128
TOKENS = 4096
N_DP = 16


def draw_tokens(key, part):
    keys = jax.random.split(jax.random.fold_in(key, 11), 3)
    base = jax.random.normal(keys[0], (TOKENS, D), jnp.float32)
    row_scale = jnp.exp(jax.random.uniform(keys[1], (TOKENS, 1), jnp.float32, math.log(0.3), math.log(3.0)))
    col_scale = jnp.exp(jax.random.uniform(keys[2], (1, D), jnp.float32, math.log(0.5), math.log(2.0)))
    return jnp.clip(base * row_scale * col_scale, -24.0, 24.0).astype(jnp.bfloat16)


def with_spikes(values, rng, source, target, parts, factor):
    def block_of(position):
        return (jnp.arange(values.shape[position]) // (values.shape[position] // parts)).reshape((-1,) + (1,) * (values.ndim - 1 - position))

    first = jax.random.permutation(rng, parts)[block_of(target)]
    other_side = (block_of(target) + parts // 2) % parts
    return jnp.where((block_of(source) == first) | (block_of(source) == other_side), factor * values, values)


def shard_levels(stream_key, shape, shards, smallest, high):
    factor_of = 1.0
    for dim, parts in shards:
        draws = jax.random.uniform(jax.random.fold_in(jax.random.fold_in(stream_key, 6), dim), (parts,), jnp.float32, smallest / len(shards), high / len(shards))
        factor_of = factor_of * jnp.repeat(jnp.exp(draws), shape[dim] // parts).reshape((-1,) + (1,) * (len(shape) - 1 - dim))
    return factor_of


def split_up(amount, total, bound, lean):
    weights = [(1 << 20) // math.isqrt(rank ** lean) + 1 for rank in range(2, amount + 1)]
    rest, given = total - bound - (amount - 1), [1] * (amount - 1)
    while rest > 0:
        candidates = [i for i in range(amount - 1) if given[i] < bound]
        mass, remaining = sum([weights[i] for i in candidates]), rest
        for i in candidates:
            extra = min(bound - given[i], max(1, remaining * weights[i] // mass), rest)
            given[i] = given[i] + extra
            rest = rest - extra
    return np.array([bound] + given)


def uneven_parts(key, number_of, total, reach, skew):
    if number_of == 2:
        one = jax.random.randint(key, (), max(1, total - reach), min(reach, total - 1) + 1)
        return jnp.stack([one, total - one])
    sizes = jnp.asarray(split_up(number_of, total, reach, skew), jnp.int32)
    twos = (number_of - 1) // 2
    source_of, taker = sizes[1:1 + 2 * twos:2], sizes[2:2 + 2 * twos:2]
    slack = jnp.minimum(source_of - 1, reach - taker)
    moved = jax.random.randint(jax.random.fold_in(key, 1), (twos,), 0, 1 << 20) % (slack + 1)
    sizes = sizes.at[1:1 + 2 * twos:2].set(source_of - moved).at[2:2 + 2 * twos:2].set(taker + moved)
    return sizes[jax.random.permutation(jax.random.fold_in(key, 2), number_of)]


def bell_draw(rng, dims, scale, bound, cuts=(), held_as=jnp.bfloat16):
    drawn = scale * jax.random.normal(rng, dims, jnp.float32)
    if cuts:
        drawn = drawn * shard_levels(rng, dims, cuts, -0.22, 0.18)
    return jnp.clip(drawn, -bound, bound).astype(held_as)


def bell_draw_with(stream_key, shape, deviation, most, cuts, heavy, kind=jnp.bfloat16):
    values = deviation * jax.random.normal(stream_key, shape, jnp.float32)
    if cuts:
        values = values * shard_levels(stream_key, shape, cuts, -0.22, 0.18)
    return jnp.clip(with_spikes(values, jax.random.fold_in(stream_key, 3), *heavy), -most, most).astype(kind)


def setup_inputs(seed: int = 0) -> dict:
    arg_keys = jax.random.split(jax.random.key(seed), 11)
    return {
        "tokens": draw_tokens(jax.random.fold_in(arg_keys[10], 71), 0),
        "segment_ids": jax.vmap(lambda own: jnp.searchsorted(jnp.cumsum(uneven_parts(own, SEGS, TOK_DEV, MOST_DOC, 1)), jnp.arange(TOK_DEV), side="right"))(jax.random.split(arg_keys[1], N_DP)).reshape((N_DP, TOK_DEV)).astype(jnp.int32),
        "norm1_gain": jnp.clip(1.0 + 0.1 * jax.random.normal(arg_keys[2], (D,), jnp.float32), 0.5, 1.5),
        "in_proj": bell_draw(arg_keys[3], (D, 3, D), D ** -0.5, 0.1875, ((0, 16), (2, 2))),
        "conv_weight": bell_draw(arg_keys[4], (3, D), 0.6, 3.0, (), jnp.float32),
        "out_proj": bell_draw(arg_keys[5], (D, D), D ** -0.5, 0.1875, ((0, 16), (1, 2))),
        "norm2_gain": jnp.clip(1.0 + 0.1 * jax.random.normal(arg_keys[6], (D,), jnp.float32), 0.5, 1.5),
        "gate_up": bell_draw(arg_keys[7], (D, 2, FF), D ** -0.5, 0.1875, ((0, 16), (2, 2))),
        "down_proj": bell_draw(arg_keys[8], (D, FF), (FF // 4) ** -0.5, 0.1875, ((0, 16), (1, 2))),
        "cotangent": bell_draw_with(arg_keys[9], (TOKENS, D), 1.0, 6.0, ((0, 32),), (0, 1, 32, 2.75)),
    }


EPSILON = 1e-05

def matmul(form, left, right):
    return jnp.einsum(form, left.astype(jnp.float32), right.astype(jnp.float32), precision=lax.Precision.HIGHEST)

def rms_forward(values, norm_gain):
    factor = lax.rsqrt(lax.optimization_barrier(jnp.mean(values * values, axis=-1, keepdims=True)) + EPSILON)
    return (values * factor * norm_gain, factor)

def rms_backward(values, factor, norm_gain, upstream):
    scaled = upstream * norm_gain
    result = factor * scaled - values * (factor * factor * factor) * lax.optimization_barrier(jnp.mean(scaled * values, axis=-1, keepdims=True))
    return (result, lax.optimization_barrier(jnp.sum(upstream * values * factor, axis=0)))

def lagged(values, offset):
    return jnp.concatenate([jnp.zeros((offset, values.shape[1]), values.dtype), values[:-offset]], axis=0)

def leading(values, offset):
    return jnp.concatenate([values[offset:], jnp.zeros((offset, values.shape[1]), values.dtype)], axis=0)

def reset_masks(segment):
    same_one = jnp.concatenate([jnp.zeros((1,), jnp.bool_), segment[1:] == segment[:-1]])
    same_two = jnp.concatenate([jnp.zeros((2,), jnp.bool_), segment[2:] == segment[:-2]])
    return (same_one.astype(jnp.float32)[:, None], same_two.astype(jnp.float32)[:, None])

def conv_forward(values, kernel, mask_one, mask_two):
    return kernel[0] * values + kernel[1] * mask_one * lagged(values, 1) + kernel[2] * mask_two * lagged(values, 2)

def conv_backward(values, upstream, kernel, mask_one, mask_two):
    result = kernel[0] * upstream + leading(kernel[1] * mask_one * upstream, 1) + leading(kernel[2] * mask_two * upstream, 2)
    grads = jnp.stack([lax.optimization_barrier(jnp.sum(upstream * values, axis=0)), lax.optimization_barrier(jnp.sum(upstream * mask_one * lagged(values, 1), axis=0)), lax.optimization_barrier(jnp.sum(upstream * mask_two * lagged(values, 2), axis=0))])
    return (result, grads)

def block_pass(seq_tokens, segment, seq_cotangent, norm1_gain, in_proj, conv_weight, out_proj, norm2_gain, gate_up, down_proj):
    inputs = seq_tokens.astype(jnp.float32)
    mask_one, mask_two = reset_masks(segment)
    normed_one, factor_one = rms_forward(inputs, norm1_gain)
    normed_one = normed_one.astype(jnp.bfloat16)
    projected = matmul('td,djc->jtc', normed_one, in_proj)
    b_part, c_part, x_part = (projected[0], projected[1], projected[2])
    mixed_in = b_part * x_part
    conv_out = conv_forward(mixed_in, conv_weight, mask_one, mask_two)
    gated = (c_part * conv_out).astype(jnp.bfloat16)
    resid = inputs + matmul('tc,dc->td', gated, out_proj)
    normed_two, factor_two = rms_forward(resid, norm2_gain)
    normed_two = normed_two.astype(jnp.bfloat16)
    lifted = matmul('td,djf->jtf', normed_two, gate_up)
    gate_lin, up_lin = (lifted[0], lifted[1])
    sigmoid_gate = jax.nn.sigmoid(gate_lin)
    activ = gate_lin * sigmoid_gate
    hidden = (activ * up_lin).astype(jnp.bfloat16)
    block_out = resid + matmul('tf,df->td', hidden, down_proj)
    grad_down = matmul('td,tf->df', seq_cotangent, hidden)
    back_hidden = matmul('td,df->tf', seq_cotangent, down_proj)
    back_gate = (back_hidden * up_lin * sigmoid_gate * (1.0 + gate_lin * (1.0 - sigmoid_gate))).astype(jnp.bfloat16)
    back_up = (back_hidden * activ).astype(jnp.bfloat16)
    back_lifted = jnp.stack([back_gate, back_up])
    grad_gate_up = matmul('td,jtf->djf', normed_two, back_lifted)
    back_normed2 = matmul('jtf,djf->td', back_lifted, gate_up)
    resid_part, grad_norm2 = rms_backward(resid, factor_two, norm2_gain, back_normed2)
    back_resid = seq_cotangent.astype(jnp.float32) + resid_part
    back_resid16 = back_resid.astype(jnp.bfloat16)
    grad_out_proj = matmul('td,tc->dc', back_resid16, gated)
    back_gated = matmul('td,dc->tc', back_resid16, out_proj)
    back_c = back_gated * conv_out
    back_conv = back_gated * c_part
    back_mixed, grad_conv = conv_backward(mixed_in, back_conv, conv_weight, mask_one, mask_two)
    back_proj = jnp.stack([back_mixed * x_part, back_c, back_mixed * b_part]).astype(jnp.bfloat16)
    grad_in_proj = matmul('td,jtc->djc', normed_one, back_proj)
    back_normed1 = matmul('jtc,djc->td', back_proj, in_proj)
    input_part, grad_norm1 = rms_backward(inputs, factor_one, norm1_gain, back_normed1)
    grad_tokens = back_resid + input_part
    return ((block_out, grad_tokens), (grad_norm1, grad_in_proj, grad_conv, grad_out_proj, grad_norm2, grad_gate_up, grad_down))

def reference(tokens, segment_ids, norm1_gain, in_proj, conv_weight, out_proj, norm2_gain, gate_up, down_proj, cotangent):
    blocks = (tokens.reshape(N_DP, TOK_DEV, D), segment_ids, cotangent.reshape(N_DP, TOK_DEV, D))
    start = (jnp.zeros((D,), jnp.float32), jnp.zeros((D, 3, D), jnp.float32), jnp.zeros((3, D), jnp.float32), jnp.zeros((D, D), jnp.float32), jnp.zeros((D,), jnp.float32), jnp.zeros((D, 2, FF), jnp.float32), jnp.zeros((D, FF), jnp.float32))

    def layer_step(totals, inputs):
        seq_tokens, segment, seq_cotangent = inputs
        outputs, grads = block_pass(seq_tokens, segment, seq_cotangent, norm1_gain, in_proj, conv_weight, out_proj, norm2_gain, gate_up, down_proj)
        return (jax.tree.map(lambda first_term, other_term: first_term + other_term, totals, grads), outputs)
    totals, outputs = lax.scan(layer_step, start, blocks)
    block_out = outputs[0].reshape(TOKENS, D)
    grad_tokens = outputs[1].reshape(TOKENS, D)
    return (block_out, grad_tokens, totals[0], totals[1], totals[2], totals[3], totals[4], totals[5], totals[6])
```

```python
import functools

import jax
import jax.numpy as jnp
from jax import lax
from jax.experimental import pallas as pl
from jax.experimental.pallas import tpu as pltpu
from jax.sharding import PartitionSpec as P

EPSILON = 1e-05


def rms_forward(values, norm_gain):
    factor = lax.rsqrt(jnp.mean(values * values, axis=-1, keepdims=True) + EPSILON)
    return (values * factor * norm_gain, factor)


def rms_backward(values, factor, norm_gain, upstream):
    scaled = upstream * norm_gain
    result = factor * scaled - values * (factor * factor * factor) * jnp.mean(
        scaled * values, axis=-1, keepdims=True
    )
    return (result, jnp.sum(upstream * values * factor, axis=0))


MESH = pl.DeviceIdType.MESH


def chip_at(pos, chips):
    back = pos // (chips // 2)
    return (1 - back) * 2 * pos + back * (2 * (chips - 1 - pos) + 1)


def ring_place(chips):
    me = lax.axis_index("dp")
    core, chip = me % 2, me // 2
    odd = chip % 2
    pos = (1 - odd) * (chip // 2) + odd * (chips - 1 - chip // 2)

    def owner(steps):
        return chip_at((pos + steps + 2 * chips) % chips, chips)

    return me, core, chip, owner


def greet(others):
    barrier = pltpu.get_barrier_semaphore()
    for other in others:
        pl.semaphore_signal(barrier, inc=1, device_id={"dp": other}, device_id_type=MESH)
    pl.semaphore_wait(barrier, len(others))


def gather_kernel(chips, ways, *refs):
    count = len(ways)
    ins, outs = refs[:count], refs[count : 2 * count]
    own_sem, send_sem, recv_sem, hand_sem, take_sem = refs[2 * count :]
    me, core, chip, owner = ring_place(chips)
    partner = chip * 2 + 1 - core
    nexts = {way: owner(way) * 2 + core for way in (1, -1)}
    greet((nexts[1], nexts[-1], partner))
    own, started = [], []
    arriving = [None] * count
    for step in range(chips):
        for i, way in enumerate(ways):
            slot = owner(-way * step) * 2 + core
            if step:
                arriving[i].wait_recv()
            source = outs[i].at[slot] if step else ins[i]
            if step < chips - 1:
                ring = pltpu.make_async_remote_copy(
                    src_ref=source,
                    dst_ref=outs[i].at[slot],
                    send_sem=send_sem.at[i, step],
                    recv_sem=recv_sem.at[i, step],
                    device_id={"dp": nexts[way]},
                    device_id_type=MESH,
                )
                ring.start()
                arriving[i] = ring
                started.append((ring, False))
            hand = pltpu.make_async_remote_copy(
                src_ref=source,
                dst_ref=outs[i].at[slot],
                send_sem=hand_sem.at[i, step],
                recv_sem=take_sem.at[i, step],
                device_id={"dp": partner},
                device_id_type=MESH,
            )
            hand.start()
            started.append((hand, True))
            if step == 0:
                keep = pltpu.make_async_copy(ins[i], outs[i].at[me], own_sem.at[i])
                keep.start()
                own.append(keep)
    for copy, handed in started:
        copy.wait_send()
        if handed:
            copy.wait_recv()
    for keep in own:
        keep.wait()


def gather_all(shards, ways, ranks):
    chips, count = ranks // 2, len(shards)
    dma = pltpu.SemaphoreType.DMA
    gathered = pl.pallas_call(
        functools.partial(gather_kernel, chips, ways),
        out_shape=[jax.ShapeDtypeStruct((ranks,) + s.shape, s.dtype) for s in shards],
        in_specs=[pl.BlockSpec(memory_space=pltpu.VMEM)] * count,
        out_specs=[pl.BlockSpec(memory_space=pl.ANY)] * count,
        scratch_shapes=[
            dma((count,)),
            dma((count, chips - 1)),
            dma((count, chips - 1)),
            dma((count, chips)),
            dma((count, chips)),
        ],
        compiler_params=pltpu.CompilerParams(collective_id=1, has_side_effects=True),
    )(*shards)
    return [g.reshape(ranks * s.shape[0], s.shape[1]) for g, s in zip(gathered, shards)]


def scatter_kernel(chips, ways, *refs):
    count = len(ways)
    ins, outs = refs[:count], refs[count : 2 * count]
    mine = refs[2 * count : 3 * count]
    theirs = refs[3 * count : 4 * count]
    moving = refs[4 * count : 5 * count]
    load_sem, send_sem, recv_sem, hand_sem, take_sem = refs[5 * count :]
    me, core, chip, owner = ring_place(chips)
    partner = chip * 2 + 1 - core
    nexts = {way: owner(way) * 2 + core for way in (1, -1)}
    greet((nexts[1], nexts[-1], partner))
    loads, swaps = {}, {}
    for step in range(chips):
        for i, way in enumerate(ways):
            target = owner(-way * (step + 1))
            load = pltpu.make_async_copy(
                ins[i].at[target * 2 + core], mine[i].at[step], load_sem.at[i, step]
            )
            load.start()
            loads[i, step] = load
            swap = pltpu.make_async_remote_copy(
                src_ref=ins[i].at[target * 2 + 1 - core],
                dst_ref=theirs[i].at[step],
                send_sem=hand_sem.at[i, step],
                recv_sem=take_sem.at[i, step],
                device_id={"dp": partner},
                device_id_type=MESH,
            )
            swap.start()
            swaps[i, step] = swap
    hops = {}
    for step in range(chips):
        for i, way in enumerate(ways):
            rows = ins[i].shape[1]
            tile = min(rows, 16)
            loads[i, step].wait()
            swaps[i, step].wait_recv()
            if step:
                hops[i, step - 1].wait_recv()
            last = step == chips - 1
            into = outs[i] if last else (moving[i].at[step - 1] if step else mine[i].at[step])

            @pl.loop(0, rows // tile)
            def _(block):
                span = pl.ds(pl.multiple_of(block * tile, tile), tile)
                total = mine[i][step, span, :].astype(jnp.float32) + theirs[i][
                    step, span, :
                ].astype(jnp.float32)
                if step:
                    total = total + moving[i][step - 1, span, :].astype(jnp.float32)
                into[span, :] = total.astype(into.dtype)

            if not last:
                hop = pltpu.make_async_remote_copy(
                    src_ref=into,
                    dst_ref=moving[i].at[step],
                    send_sem=send_sem.at[i, step],
                    recv_sem=recv_sem.at[i, step],
                    device_id={"dp": nexts[way]},
                    device_id_type=MESH,
                )
                hop.start()
                hops[i, step] = hop
    for copy in list(hops.values()) + list(swaps.values()):
        copy.wait_send()


def scatter_all(grads, ways, ranks):
    chips, count = ranks // 2, len(grads)
    grads = [g.reshape(ranks, g.shape[0] // ranks, g.shape[1]) for g in grads]
    dma = pltpu.SemaphoreType.DMA
    blocks = [g.shape[1:] for g in grads]
    return pl.pallas_call(
        functools.partial(scatter_kernel, chips, ways),
        out_shape=[jax.ShapeDtypeStruct(b, jnp.float32) for b in blocks],
        in_specs=[pl.BlockSpec(memory_space=pl.ANY)] * count,
        out_specs=[pl.BlockSpec(memory_space=pltpu.VMEM)] * count,
        scratch_shapes=[pltpu.VMEM((chips,) + b, jnp.bfloat16) for b in blocks]
        + [pltpu.VMEM((chips,) + b, jnp.bfloat16) for b in blocks]
        + [pltpu.VMEM((chips - 1,) + b, jnp.bfloat16) for b in blocks]
        + [
            dma((count, chips)),
            dma((count, chips - 1)),
            dma((count, chips - 1)),
            dma((count, chips)),
            dma((count, chips)),
        ],
        compiler_params=pltpu.CompilerParams(
            collective_id=2, has_side_effects=True, vmem_limit_bytes=56 * 1024 * 1024
        ),
    )(*grads)


def both(values):
    other = lax.ppermute(values, "tensor", [(0, 1), (1, 0)])
    return jnp.concatenate([values, other], axis=0)


def halves_sum(terms):
    half = terms.shape[0] // 2
    sent = lax.ppermute(terms[half:].astype(jnp.bfloat16), "tensor", [(0, 1), (1, 0)])
    return terms[:half] + sent.astype(jnp.float32)


def reset_masks(segment):
    same_one = jnp.concatenate([jnp.zeros((1,), jnp.bool_), segment[1:] == segment[:-1]])
    same_two = jnp.concatenate([jnp.zeros((2,), jnp.bool_), segment[2:] == segment[:-2]])
    masks = jnp.stack([same_one, same_two]).astype(jnp.float32)
    half = segment.shape[0] // 2
    turned = jnp.concatenate([masks[:, half:], masks[:, :half]], axis=1)
    masks = jnp.where(lax.axis_index("tensor") == 0, masks, turned)
    return (masks[0][:, None], masks[1][:, None])


def turn(values, offset):
    return jnp.concatenate([values[-offset:], values[:-offset]], axis=0)


def dot(left, right, dims):
    return lax.dot_general(left, right, (dims, ((), ())), preferred_element_type=jnp.float32)


GATHER_WAYS = (1, -1, -1, -1)


def local(
    tokens,
    segment_ids,
    norm1_gain,
    in_proj,
    conv_weight,
    out_proj,
    norm2_gain,
    gate_up,
    down_proj,
    cotangent,
    *,
    ranks,
):
    rows, _, channels = in_proj.shape
    hidden_units = gate_up.shape[2]
    lift_full, in_full, out_full, down_full = gather_all(
        [
            gate_up.reshape(rows, 2 * hidden_units),
            in_proj.reshape(rows, 3 * channels),
            out_proj,
            down_proj,
        ],
        GATHER_WAYS,
        ranks,
    )
    offset = lax.axis_index("tensor") * channels
    kernel = lax.dynamic_slice_in_dim(conv_weight, offset, channels, 1)
    mask_one, mask_two = reset_masks(segment_ids[0])
    inputs = tokens.astype(jnp.float32)
    normed_one, factor_one = rms_forward(inputs, norm1_gain)
    rows_one = both(normed_one.astype(jnp.bfloat16))
    cot_rows = both(cotangent)
    projected = dot(rows_one, in_full, ((1,), (0,)))
    b_part = projected[:, :channels]
    c_part = projected[:, channels : 2 * channels]
    x_part = projected[:, 2 * channels :]
    mixed_in = b_part * x_part
    mixed_one = mask_one * turn(mixed_in, 1)
    mixed_two = mask_two * turn(mixed_in, 2)
    conv_out = kernel[0] * mixed_in + kernel[1] * mixed_one + kernel[2] * mixed_two
    gated = (c_part * conv_out).astype(jnp.bfloat16)
    resid = inputs + halves_sum(dot(gated, out_full, ((1,), (1,))))
    normed_two, factor_two = rms_forward(resid, norm2_gain)
    rows_two = both(normed_two.astype(jnp.bfloat16))
    lifted = dot(rows_two, lift_full, ((1,), (0,)))
    gate_lin, up_lin = lifted[:, :hidden_units], lifted[:, hidden_units:]
    sigmoid_gate = jax.nn.sigmoid(gate_lin)
    activ = gate_lin * sigmoid_gate
    hidden = (activ * up_lin).astype(jnp.bfloat16)
    block_out = resid + halves_sum(dot(hidden, down_full, ((1,), (1,))))
    grad_down = dot(cot_rows, hidden, ((0,), (0,))).astype(jnp.bfloat16)
    back_hidden = dot(cot_rows, down_full, ((1,), (0,)))
    back_gate = (
        back_hidden * up_lin * sigmoid_gate * (1.0 + gate_lin * (1.0 - sigmoid_gate))
    ).astype(jnp.bfloat16)
    back_up = (back_hidden * activ).astype(jnp.bfloat16)
    back_lifted = jnp.concatenate([back_gate, back_up], axis=1)
    grad_lift = dot(rows_two, back_lifted, ((0,), (0,))).astype(jnp.bfloat16)
    back_normed2 = halves_sum(dot(back_lifted, lift_full, ((1,), (1,))))
    resid_part, gain_two = rms_backward(resid, factor_two, norm2_gain, back_normed2)
    back_resid = cotangent.astype(jnp.float32) + resid_part
    resid_rows = both(back_resid.astype(jnp.bfloat16))
    grad_out = dot(resid_rows, gated, ((0,), (0,))).astype(jnp.bfloat16)
    back_gated = dot(resid_rows, out_full, ((1,), (0,)))
    back_c = back_gated * conv_out
    back_conv = back_gated * c_part
    back_mixed = (
        kernel[0] * back_conv
        + turn(kernel[1] * mask_one * back_conv, -1)
        + turn(kernel[2] * mask_two * back_conv, -2)
    )
    conv_local = jnp.stack(
        [
            jnp.sum(back_conv * mixed_in, axis=0),
            jnp.sum(back_conv * mixed_one, axis=0),
            jnp.sum(back_conv * mixed_two, axis=0),
        ]
    )
    back_proj = jnp.concatenate(
        [back_mixed * x_part, back_c, back_mixed * b_part], axis=1
    ).astype(jnp.bfloat16)
    grad_in = dot(rows_one, back_proj, ((0,), (0,))).astype(jnp.bfloat16)
    back_normed1 = halves_sum(dot(back_proj, in_full, ((1,), (1,))))
    input_part, gain_one = rms_backward(inputs, factor_one, norm1_gain, back_normed1)
    grad_tokens = back_resid + input_part
    conv_placed = lax.dynamic_update_slice_in_dim(
        jnp.zeros(conv_weight.shape, jnp.float32), conv_local, offset, 1
    )
    small = jnp.concatenate([gain_one[None], gain_two[None], conv_placed], axis=0)
    small = lax.psum(small, ("dp", "tensor"))
    lift_shard, in_shard, out_shard, down_shard = scatter_all(
        [grad_lift, grad_in, grad_out, grad_down], GATHER_WAYS, ranks
    )
    return (
        block_out,
        grad_tokens,
        small[0],
        in_shard.reshape(in_proj.shape),
        small[2:],
        out_shard,
        small[1],
        lift_shard.reshape(gate_up.shape),
        down_shard,
    )


def solution(mesh):
    placed = (
        P(("dp", "tensor"), None),
        P("dp", None),
        P(),
        P("dp", None, "tensor"),
        P(),
        P("dp", "tensor"),
        P(),
        P("dp", None, "tensor"),
        P("dp", "tensor"),
        P(("dp", "tensor"), None),
    )
    return jax.shard_map(
        functools.partial(local, ranks=mesh.shape["dp"]),
        mesh=mesh,
        in_specs=placed,
        out_specs=(
            P(("dp", "tensor"), None),
            P(("dp", "tensor"), None),
            P(),
            P("dp", None, "tensor"),
            P(),
            P("dp", "tensor"),
            P(),
            P("dp", None, "tensor"),
            P("dp", "tensor"),
        ),
        check_vma=False,
    )
```

```python
import functools

import jax
import jax.numpy as jnp
from jax import lax
from jax.experimental import pallas as pl
from jax.experimental.pallas import tpu as pltpu
from jax.sharding import PartitionSpec as P

EPSILON = 1e-05


def rms_forward(values, norm_gain):
    factor = lax.rsqrt(jnp.mean(values * values, axis=-1, keepdims=True) + EPSILON)
    return (values * factor * norm_gain, factor)


def rms_backward(values, factor, norm_gain, upstream):
    scaled = upstream * norm_gain
    result = factor * scaled - values * (factor * factor * factor) * jnp.mean(
        scaled * values, axis=-1, keepdims=True
    )
    return (result, jnp.sum(upstream * values * factor, axis=0))


MESH = pl.DeviceIdType.MESH


def chip_at(pos, chips):
    back = pos // (chips // 2)
    return (1 - back) * 2 * pos + back * (2 * (chips - 1 - pos) + 1)


def ring_place(chips):
    me = lax.axis_index("dp")
    core, chip = me % 2, me // 2
    odd = chip % 2
    pos = (1 - odd) * (chip // 2) + odd * (chips - 1 - chip // 2)

    def owner(steps):
        return chip_at((pos + steps + 2 * chips) % chips, chips)

    return me, core, chip, owner


def greet(others):
    barrier = pltpu.get_barrier_semaphore()
    peer = 1 - lax.axis_index("tensor")
    pl.semaphore_signal(barrier, inc=1, device_id={"tensor": peer}, device_id_type=MESH)
    for other in others:
        pl.semaphore_signal(barrier, inc=1, device_id={"dp": other}, device_id_type=MESH)
    pl.semaphore_wait(barrier, len(others) + 1)


def across(source, into, send_sem, recv_sem):
    return pltpu.make_async_remote_copy(
        src_ref=source,
        dst_ref=into,
        send_sem=send_sem,
        recv_sem=recv_sem,
        device_id={"tensor": 1 - lax.axis_index("tensor")},
        device_id_type=MESH,
    )


def gather_kernel(chips, ways, *refs):
    count = len(ways)
    pairs = (len(refs) - 2 * count - 7) // 2
    swaps_in, refs = refs[:pairs], refs[pairs:]
    ins, refs = refs[:count], refs[count:]
    swaps_out, refs = refs[:pairs], refs[pairs:]
    outs = refs[:count]
    own_sem, send_sem, recv_sem, hand_sem, take_sem, out_sem, in_sem = refs[count:]
    me, core, chip, owner = ring_place(chips)
    partner = chip * 2 + 1 - core
    nexts = {way: owner(way) * 2 + core for way in (1, -1)}
    greet((nexts[1], nexts[-1], partner))
    own, started = [], []
    for i in range(pairs):
        swap = across(swaps_in[i], swaps_out[i], out_sem.at[i], in_sem.at[i])
        swap.start()
        started.append((swap, True))
    arriving = [None] * count
    for step in range(chips):
        for i, way in enumerate(ways):
            slot = owner(-way * step) * 2 + core
            if step:
                arriving[i].wait_recv()
            source = outs[i].at[slot] if step else ins[i]
            if step < chips - 1:
                ring = pltpu.make_async_remote_copy(
                    src_ref=source,
                    dst_ref=outs[i].at[slot],
                    send_sem=send_sem.at[i, step],
                    recv_sem=recv_sem.at[i, step],
                    device_id={"dp": nexts[way]},
                    device_id_type=MESH,
                )
                ring.start()
                arriving[i] = ring
                started.append((ring, False))
            hand = pltpu.make_async_remote_copy(
                src_ref=source,
                dst_ref=outs[i].at[slot],
                send_sem=hand_sem.at[i, step],
                recv_sem=take_sem.at[i, step],
                device_id={"dp": partner},
                device_id_type=MESH,
            )
            hand.start()
            started.append((hand, True))
            if step == 0:
                keep = pltpu.make_async_copy(ins[i], outs[i].at[me], own_sem.at[i])
                keep.start()
                own.append(keep)
    for copy, handed in started:
        copy.wait_send()
        if handed:
            copy.wait_recv()
    for keep in own:
        keep.wait()


def gather_all(swapped, shards, ways, ranks):
    chips, count, pairs = ranks // 2, len(shards), len(swapped)
    dma = pltpu.SemaphoreType.DMA
    outs = pl.pallas_call(
        functools.partial(gather_kernel, chips, ways),
        out_shape=[jax.ShapeDtypeStruct(s.shape, s.dtype) for s in swapped]
        + [jax.ShapeDtypeStruct((ranks,) + s.shape, s.dtype) for s in shards],
        in_specs=[pl.BlockSpec(memory_space=pltpu.VMEM)] * (pairs + count),
        out_specs=[pl.BlockSpec(memory_space=pltpu.VMEM)] * pairs
        + [pl.BlockSpec(memory_space=pl.ANY)] * count,
        scratch_shapes=[
            dma((count,)),
            dma((count, chips - 1)),
            dma((count, chips - 1)),
            dma((count, chips)),
            dma((count, chips)),
            dma((pairs,)),
            dma((pairs,)),
        ],
        compiler_params=pltpu.CompilerParams(collective_id=1, has_side_effects=True),
    )(*swapped, *shards)
    full = [g.reshape(ranks * s.shape[0], s.shape[1]) for g, s in zip(outs[pairs:], shards)]
    return outs[:pairs], full


def scatter_kernel(chips, ways, *refs):
    count = len(ways)
    small_in, row_in, refs = refs[0], refs[1], refs[2:]
    ins, refs = refs[:count], refs[count:]
    small_out, row_out, refs = refs[0], refs[1], refs[2:]
    outs, refs = refs[:count], refs[count:]
    mine = refs[:count]
    theirs = refs[count : 2 * count]
    moving = refs[2 * count : 3 * count]
    smalls, folded, folded_other, refs = *refs[3 * count : 3 * count + 3], refs[3 * count + 3 :]
    load_sem, send_sem, recv_sem, hand_sem, take_sem, own_sem, out_sem, in_sem = refs[:8]
    small_send, small_recv, small_hand, small_take = refs[8:]
    me, core, chip, owner = ring_place(chips)
    partner = chip * 2 + 1 - core
    nexts = {way: owner(way) * 2 + core for way in (1, -1)}
    greet((nexts[1], nexts[-1], partner))
    row_swap = across(row_in, row_out, out_sem.at[0], in_sem.at[0])
    row_swap.start()
    keep = pltpu.make_async_copy(small_in, smalls.at[me], own_sem)
    keep.start()
    small_hops, small_hands = [], []
    loads, swaps = {}, {}
    for step in range(chips):
        for i, way in enumerate(ways):
            target = owner(-way * (step + 1))
            load = pltpu.make_async_copy(
                ins[i].at[target * 2 + core], mine[i].at[step], load_sem.at[i, step]
            )
            load.start()
            loads[i, step] = load
            swap = pltpu.make_async_remote_copy(
                src_ref=ins[i].at[target * 2 + 1 - core],
                dst_ref=theirs[i].at[step],
                send_sem=hand_sem.at[i, step],
                recv_sem=take_sem.at[i, step],
                device_id={"dp": partner},
                device_id_type=MESH,
            )
            swap.start()
            swaps[i, step] = swap
    hops = {}
    for step in range(chips):
        slot = owner(-step) * 2 + core
        if step:
            small_hops[step - 1].wait_recv()
        source = smalls.at[slot] if step else small_in
        if step < chips - 1:
            ring = pltpu.make_async_remote_copy(
                src_ref=source,
                dst_ref=smalls.at[slot],
                send_sem=small_send.at[step],
                recv_sem=small_recv.at[step],
                device_id={"dp": nexts[1]},
                device_id_type=MESH,
            )
            ring.start()
            small_hops.append(ring)
        hand = pltpu.make_async_remote_copy(
            src_ref=source,
            dst_ref=smalls.at[slot],
            send_sem=small_hand.at[step],
            recv_sem=small_take.at[step],
            device_id={"dp": partner},
            device_id_type=MESH,
        )
        hand.start()
        small_hands.append(hand)
        if step == chips - 1:
            keep.wait()
            for hand in small_hands:
                hand.wait_recv()
            folded[...] = lax.fori_loop(
                1, 2 * chips, lambda k, total: total + smalls[k], smalls[0]
            )
            fold_swap = across(folded, folded_other, out_sem.at[1], in_sem.at[1])
            fold_swap.start()
        for i, way in enumerate(ways):
            rows = ins[i].shape[1]
            tile = min(rows, 16)
            loads[i, step].wait()
            swaps[i, step].wait_recv()
            if step:
                hops[i, step - 1].wait_recv()
            last = step == chips - 1
            into = outs[i] if last else (moving[i].at[step - 1] if step else mine[i].at[step])

            @pl.loop(0, rows // tile)
            def _(block):
                span = pl.ds(pl.multiple_of(block * tile, tile), tile)
                total = mine[i][step, span, :].astype(jnp.float32) + theirs[i][
                    step, span, :
                ].astype(jnp.float32)
                if step:
                    total = total + moving[i][step - 1, span, :].astype(jnp.float32)
                into[span, :] = total.astype(into.dtype)

            if not last:
                hop = pltpu.make_async_remote_copy(
                    src_ref=into,
                    dst_ref=moving[i].at[step],
                    send_sem=send_sem.at[i, step],
                    recv_sem=recv_sem.at[i, step],
                    device_id={"dp": nexts[way]},
                    device_id_type=MESH,
                )
                hop.start()
                hops[i, step] = hop
    fold_swap.wait()
    small_out[...] = folded[...] + folded_other[...]
    row_swap.wait()
    for copy in list(hops.values()) + list(swaps.values()) + small_hops + small_hands:
        copy.wait_send()


def scatter_all(small, rows, grads, ways, ranks):
    chips, count = ranks // 2, len(grads)
    grads = [g.reshape(ranks, g.shape[0] // ranks, g.shape[1]) for g in grads]
    dma = pltpu.SemaphoreType.DMA
    blocks = [g.shape[1:] for g in grads]
    return pl.pallas_call(
        functools.partial(scatter_kernel, chips, ways),
        out_shape=[jax.ShapeDtypeStruct(v.shape, v.dtype) for v in (small, rows)]
        + [jax.ShapeDtypeStruct(b, jnp.float32) for b in blocks],
        in_specs=[pl.BlockSpec(memory_space=pltpu.VMEM)] * 2
        + [pl.BlockSpec(memory_space=pl.ANY)] * count,
        out_specs=[pl.BlockSpec(memory_space=pltpu.VMEM)] * (count + 2),
        scratch_shapes=[pltpu.VMEM((chips,) + b, jnp.bfloat16) for b in blocks]
        + [pltpu.VMEM((chips,) + b, jnp.bfloat16) for b in blocks]
        + [pltpu.VMEM((chips - 1,) + b, jnp.bfloat16) for b in blocks]
        + [pltpu.VMEM((ranks,) + small.shape, small.dtype)]
        + [pltpu.VMEM(small.shape, small.dtype)] * 2
        + [
            dma((count, chips)),
            dma((count, chips - 1)),
            dma((count, chips - 1)),
            dma((count, chips)),
            dma((count, chips)),
            dma,
            dma((2,)),
            dma((2,)),
            dma((chips - 1,)),
            dma((chips - 1,)),
            dma((chips,)),
            dma((chips,)),
        ],
        compiler_params=pltpu.CompilerParams(
            collective_id=2, has_side_effects=True, vmem_limit_bytes=56 * 1024 * 1024
        ),
    )(small, rows, *grads)


def both(values):
    other = lax.ppermute(values, "tensor", [(0, 1), (1, 0)])
    return jnp.concatenate([values, other], axis=0)


def halves_sum(terms):
    half = terms.shape[0] // 2
    sent = lax.ppermute(terms[half:].astype(jnp.bfloat16), "tensor", [(0, 1), (1, 0)])
    return terms[:half] + sent.astype(jnp.float32)


def reset_masks(segment):
    same_one = jnp.concatenate([jnp.zeros((1,), jnp.bool_), segment[1:] == segment[:-1]])
    same_two = jnp.concatenate([jnp.zeros((2,), jnp.bool_), segment[2:] == segment[:-2]])
    masks = jnp.stack([same_one, same_two]).astype(jnp.float32)
    half = segment.shape[0] // 2
    turned = jnp.concatenate([masks[:, half:], masks[:, :half]], axis=1)
    masks = jnp.where(lax.axis_index("tensor") == 0, masks, turned)
    return (masks[0][:, None], masks[1][:, None])


def turn(values, offset):
    return jnp.concatenate([values[-offset:], values[:-offset]], axis=0)


def dot(left, right, dims):
    return lax.dot_general(left, right, (dims, ((), ())), preferred_element_type=jnp.float32)


WAYS = (-1, -1, 1, 1, -1)


def local(
    tokens,
    segment_ids,
    norm1_gain,
    in_proj,
    conv_weight,
    out_proj,
    norm2_gain,
    gate_up,
    down_proj,
    cotangent,
    *,
    ranks,
):
    rows, _, channels = in_proj.shape
    inputs = tokens.astype(jnp.float32)
    normed_one, factor_one = rms_forward(inputs, norm1_gain)
    normed_one = normed_one.astype(jnp.bfloat16)
    (normed_other, cot_other), (in_full, out_full, gate_full, up_full, down_full) = gather_all(
        [normed_one, cotangent],
        [
            in_proj.reshape(rows, 3 * channels),
            out_proj,
            gate_up[:, 0, :],
            gate_up[:, 1, :],
            down_proj,
        ],
        WAYS,
        ranks,
    )
    rows_one = jnp.concatenate([normed_one, normed_other], axis=0)
    cot_rows = jnp.concatenate([cotangent, cot_other], axis=0)
    offset = lax.axis_index("tensor") * channels
    kernel = lax.dynamic_slice_in_dim(conv_weight, offset, channels, 1)
    mask_one, mask_two = reset_masks(segment_ids[0])
    projected = dot(rows_one, in_full, ((1,), (0,)))
    b_part = projected[:, :channels]
    c_part = projected[:, channels : 2 * channels]
    x_part = projected[:, 2 * channels :]
    mixed_in = b_part * x_part
    mixed_one = mask_one * turn(mixed_in, 1)
    mixed_two = mask_two * turn(mixed_in, 2)
    conv_out = kernel[0] * mixed_in + kernel[1] * mixed_one + kernel[2] * mixed_two
    gated = (c_part * conv_out).astype(jnp.bfloat16)
    resid = inputs + halves_sum(dot(gated, out_full, ((1,), (1,))))
    normed_two, factor_two = rms_forward(resid, norm2_gain)
    rows_two = both(normed_two.astype(jnp.bfloat16))
    gate_lin = dot(rows_two, gate_full, ((1,), (0,)))
    up_lin = dot(rows_two, up_full, ((1,), (0,)))
    sigmoid_gate = jax.nn.sigmoid(gate_lin)
    activ = gate_lin * sigmoid_gate
    hidden = (activ * up_lin).astype(jnp.bfloat16)
    ffn_terms = dot(hidden, down_full, ((1,), (1,)))
    grad_down = dot(cot_rows, hidden, ((0,), (0,))).astype(jnp.bfloat16)
    back_hidden = dot(cot_rows, down_full, ((1,), (0,)))
    back_gate = (
        back_hidden * up_lin * sigmoid_gate * (1.0 + gate_lin * (1.0 - sigmoid_gate))
    ).astype(jnp.bfloat16)
    back_up = (back_hidden * activ).astype(jnp.bfloat16)
    grad_gate = dot(rows_two, back_gate, ((0,), (0,))).astype(jnp.bfloat16)
    grad_up = dot(rows_two, back_up, ((0,), (0,))).astype(jnp.bfloat16)
    back_normed2 = halves_sum(
        dot(back_gate, gate_full, ((1,), (1,))) + dot(back_up, up_full, ((1,), (1,)))
    )
    resid_part, gain_two = rms_backward(resid, factor_two, norm2_gain, back_normed2)
    back_resid = cotangent.astype(jnp.float32) + resid_part
    resid_rows = both(back_resid.astype(jnp.bfloat16))
    grad_out = dot(resid_rows, gated, ((0,), (0,))).astype(jnp.bfloat16)
    back_gated = dot(resid_rows, out_full, ((1,), (0,)))
    back_c = back_gated * conv_out
    back_conv = back_gated * c_part
    back_mixed = (
        kernel[0] * back_conv
        + turn(kernel[1] * mask_one * back_conv, -1)
        + turn(kernel[2] * mask_two * back_conv, -2)
    )
    conv_local = jnp.stack(
        [
            jnp.sum(back_conv * mixed_in, axis=0),
            jnp.sum(back_conv * mixed_one, axis=0),
            jnp.sum(back_conv * mixed_two, axis=0),
        ]
    )
    back_proj = jnp.concatenate(
        [back_mixed * x_part, back_c, back_mixed * b_part], axis=1
    ).astype(jnp.bfloat16)
    grad_in = dot(rows_one, back_proj, ((0,), (0,))).astype(jnp.bfloat16)
    back_normed1 = halves_sum(dot(back_proj, in_full, ((1,), (1,))))
    input_part, gain_one = rms_backward(inputs, factor_one, norm1_gain, back_normed1)
    grad_tokens = back_resid + input_part
    conv_placed = lax.dynamic_update_slice_in_dim(
        jnp.zeros(conv_weight.shape, jnp.float32), conv_local, offset, 1
    )
    small = jnp.concatenate(
        [gain_one[None], gain_two[None], conv_placed, jnp.zeros_like(conv_placed)], axis=0
    )
    half = ffn_terms.shape[0] // 2
    small, ffn_other, in_shard, out_shard, gate_shard, up_shard, down_shard = scatter_all(
        small,
        ffn_terms[half:].astype(jnp.bfloat16),
        [grad_in, grad_out, grad_gate, grad_up, grad_down],
        WAYS,
        ranks,
    )
    block_out = resid + (ffn_terms[:half] + ffn_other.astype(jnp.float32))
    return (
        block_out,
        grad_tokens,
        small[0],
        in_shard.reshape(in_proj.shape),
        small[2:5],
        out_shard,
        small[1],
        jnp.stack([gate_shard, up_shard], axis=1),
        down_shard,
    )


def solution(mesh):
    placed = (
        P(("dp", "tensor"), None),
        P("dp", None),
        P(),
        P("dp", None, "tensor"),
        P(),
        P("dp", "tensor"),
        P(),
        P("dp", None, "tensor"),
        P("dp", "tensor"),
        P(("dp", "tensor"), None),
    )
    return jax.shard_map(
        functools.partial(local, ranks=mesh.shape["dp"]),
        mesh=mesh,
        in_specs=placed,
        out_specs=(
            P(("dp", "tensor"), None),
            P(("dp", "tensor"), None),
            P(),
            P("dp", None, "tensor"),
            P(),
            P("dp", "tensor"),
            P(),
            P("dp", None, "tensor"),
            P("dp", "tensor"),
        ),
        check_vma=False,
    )
```

```python
import functools

import jax
import jax.numpy as jnp
from jax import lax
from jax.experimental import pallas as pl
from jax.experimental.pallas import tpu as pltpu
from jax.sharding import PartitionSpec as P

EPSILON = 1e-05


def rms_forward(values, norm_gain):
    factor = lax.rsqrt(jnp.mean(values * values, axis=-1, keepdims=True) + EPSILON)
    return (values * factor * norm_gain, factor)


def rms_backward(values, factor, norm_gain, upstream):
    scaled = upstream * norm_gain
    result = factor * scaled - values * (factor * factor * factor) * jnp.mean(
        scaled * values, axis=-1, keepdims=True
    )
    return (result, jnp.sum(upstream * values * factor, axis=0))


MESH = pl.DeviceIdType.MESH

WAYS = (-1, -1, 1, 1, -1)
BACKWARD = (1, 0, 1, 0, 0)


def chip_at(pos, chips):
    back = pos // (chips // 2)
    return (1 - back) * 2 * pos + back * (2 * (chips - 1 - pos) + 1)


def ring_place(chips):
    me = lax.axis_index("dp")
    core, chip = me % 2, me // 2
    odd = chip % 2
    pos = (1 - odd) * (chip // 2) + odd * (chips - 1 - chip // 2)

    def owner(steps):
        return chip_at((pos + steps + 2 * chips) % chips, chips)

    return me, core, chip, owner


def greet(others):
    barrier = pltpu.get_barrier_semaphore()
    peer = 1 - lax.axis_index("tensor")
    pl.semaphore_signal(barrier, inc=1, device_id={"tensor": peer}, device_id_type=MESH)
    for other in others:
        pl.semaphore_signal(barrier, inc=1, device_id={"dp": other}, device_id_type=MESH)
    pl.semaphore_wait(barrier, len(others) + 1)


def across(source, into, send_sem, recv_sem):
    return pltpu.make_async_remote_copy(
        src_ref=source,
        dst_ref=into,
        send_sem=send_sem,
        recv_sem=recv_sem,
        device_id={"tensor": 1 - lax.axis_index("tensor")},
        device_id_type=MESH,
    )


def gather_kernel(chips, ways, *refs):
    count = len(ways)
    pairs = (len(refs) - 2 * count - 7) // 2
    swaps_in, refs = refs[:pairs], refs[pairs:]
    ins, refs = refs[:count], refs[count:]
    swaps_out, refs = refs[:pairs], refs[pairs:]
    outs = refs[:count]
    own_sem, send_sem, recv_sem, hand_sem, take_sem, out_sem, in_sem = refs[count:]
    me, core, chip, owner = ring_place(chips)
    partner = chip * 2 + 1 - core
    nexts = {way: owner(way) * 2 + core for way in (1, -1)}
    greet((nexts[1], nexts[-1], partner))
    own, started = [], []
    for i in range(pairs):
        swap = across(swaps_in[i], swaps_out[i], out_sem.at[i], in_sem.at[i])
        swap.start()
        started.append((swap, True))
    arriving, direct = [None] * count, {}
    for step in range(chips):
        for i, way in enumerate(ways):
            slot = owner(-way * step) * 2 + core
            if step:
                arriving[i].wait_recv()
            source = outs[i].at[slot] if step else ins[i]
            if step < chips - 1 and not (BACKWARD[i] and step == chips - 2):
                ring = pltpu.make_async_remote_copy(
                    src_ref=source,
                    dst_ref=outs[i].at[slot],
                    send_sem=send_sem.at[i, step],
                    recv_sem=recv_sem.at[i, step],
                    device_id={"dp": nexts[way]},
                    device_id_type=MESH,
                )
                ring.start()
                arriving[i] = ring
                started.append((ring, False))
            if BACKWARD[i] and step == chips - 2:
                arriving[i] = direct[i]
            if BACKWARD[i] and step == 0:
                direct[i] = pltpu.make_async_remote_copy(
                    src_ref=source,
                    dst_ref=outs[i].at[slot],
                    send_sem=send_sem.at[i, chips - 2],
                    recv_sem=recv_sem.at[i, chips - 2],
                    device_id={"dp": nexts[-way]},
                    device_id_type=MESH,
                )
                direct[i].start()
                started.append((direct[i], False))
            hand = pltpu.make_async_remote_copy(
                src_ref=source,
                dst_ref=outs[i].at[slot],
                send_sem=hand_sem.at[i, step],
                recv_sem=take_sem.at[i, step],
                device_id={"dp": partner},
                device_id_type=MESH,
            )
            hand.start()
            started.append((hand, True))
            if step == 0:
                keep = pltpu.make_async_copy(ins[i], outs[i].at[me], own_sem.at[i])
                keep.start()
                own.append(keep)
    for copy, handed in started:
        copy.wait_send()
        if handed:
            copy.wait_recv()
    for keep in own:
        keep.wait()


def gather_all(swapped, shards, ways, ranks):
    chips, count, pairs = ranks // 2, len(shards), len(swapped)
    dma = pltpu.SemaphoreType.DMA
    outs = pl.pallas_call(
        functools.partial(gather_kernel, chips, ways),
        out_shape=[jax.ShapeDtypeStruct(s.shape, s.dtype) for s in swapped]
        + [jax.ShapeDtypeStruct((ranks,) + s.shape, s.dtype) for s in shards],
        in_specs=[pl.BlockSpec(memory_space=pltpu.VMEM)] * (pairs + count),
        out_specs=[pl.BlockSpec(memory_space=pltpu.VMEM)] * pairs
        + [pl.BlockSpec(memory_space=pl.ANY)] * count,
        scratch_shapes=[
            dma((count,)),
            dma((count, chips - 1)),
            dma((count, chips - 1)),
            dma((count, chips)),
            dma((count, chips)),
            dma((pairs,)),
            dma((pairs,)),
        ],
        compiler_params=pltpu.CompilerParams(collective_id=1, has_side_effects=True),
    )(*swapped, *shards)
    full = [g.reshape(ranks * s.shape[0], s.shape[1]) for g, s in zip(outs[pairs:], shards)]
    return outs[:pairs], full


def scatter_kernel(chips, ways, *refs):
    count = len(ways)
    small_in, row_in, refs = refs[0], refs[1], refs[2:]
    ins, refs = refs[:count], refs[count:]
    small_out, row_out, refs = refs[0], refs[1], refs[2:]
    outs, refs = refs[:count], refs[count:]
    mine = refs[:count]
    theirs = refs[count : 2 * count]
    moving = refs[2 * count : 3 * count]
    smalls, folded, folded_other, refs = *refs[3 * count : 3 * count + 3], refs[3 * count + 3 :]
    load_sem, send_sem, recv_sem, hand_sem, take_sem, own_sem, out_sem, in_sem = refs[:8]
    small_send, small_recv, small_hand, small_take = refs[8:]
    me, core, chip, owner = ring_place(chips)
    partner = chip * 2 + 1 - core
    nexts = {way: owner(way) * 2 + core for way in (1, -1)}
    greet((nexts[1], nexts[-1], partner))
    row_swap = across(row_in, row_out, out_sem.at[0], in_sem.at[0])
    row_swap.start()
    keep = pltpu.make_async_copy(small_in, smalls.at[me], own_sem)
    keep.start()
    small_hops, small_hands = [], []
    loads, swaps = {}, {}
    for step in range(chips):
        for i, way in enumerate(ways):
            target = owner(-way * (step + 1))
            load = pltpu.make_async_copy(
                ins[i].at[target * 2 + core], mine[i].at[step], load_sem.at[i, step]
            )
            load.start()
            loads[i, step] = load
            swap = pltpu.make_async_remote_copy(
                src_ref=ins[i].at[target * 2 + 1 - core],
                dst_ref=theirs[i].at[step],
                send_sem=hand_sem.at[i, step],
                recv_sem=take_sem.at[i, step],
                device_id={"dp": partner},
                device_id_type=MESH,
            )
            swap.start()
            swaps[i, step] = swap
    hops = {}
    for step in range(chips):
        slot = owner(-step) * 2 + core
        if step:
            small_hops[step - 1].wait_recv()
        source = smalls.at[slot] if step else small_in
        if step < chips - 1:
            ring = pltpu.make_async_remote_copy(
                src_ref=source,
                dst_ref=smalls.at[slot],
                send_sem=small_send.at[step],
                recv_sem=small_recv.at[step],
                device_id={"dp": nexts[1]},
                device_id_type=MESH,
            )
            ring.start()
            small_hops.append(ring)
        hand = pltpu.make_async_remote_copy(
            src_ref=source,
            dst_ref=smalls.at[slot],
            send_sem=small_hand.at[step],
            recv_sem=small_take.at[step],
            device_id={"dp": partner},
            device_id_type=MESH,
        )
        hand.start()
        small_hands.append(hand)
        if step == chips - 1:
            keep.wait()
            for hand in small_hands:
                hand.wait_recv()
            folded[...] = lax.fori_loop(
                1, 2 * chips, lambda k, total: total + smalls[k], smalls[0]
            )
            fold_swap = across(folded, folded_other, out_sem.at[1], in_sem.at[1])
            fold_swap.start()
        for i, way in enumerate(ways):
            rows = ins[i].shape[1]
            tile = min(rows, 16)
            loads[i, step].wait()
            swaps[i, step].wait_recv()
            last = step == chips - 1
            added = [step - 1] if step > BACKWARD[i] else []
            if last and BACKWARD[i]:
                added.append(0)
            for hop in added:
                hops[i, hop].wait_recv()
            into = outs[i] if last else (moving[i].at[step - 1] if added else mine[i].at[step])

            @pl.loop(0, rows // tile)
            def _(block):
                span = pl.ds(pl.multiple_of(block * tile, tile), tile)
                total = mine[i][step, span, :].astype(jnp.float32) + theirs[i][
                    step, span, :
                ].astype(jnp.float32)
                for hop in added:
                    total = total + moving[i][hop, span, :].astype(jnp.float32)
                into[span, :] = total.astype(into.dtype)

            if not last:
                hop = pltpu.make_async_remote_copy(
                    src_ref=into,
                    dst_ref=moving[i].at[step],
                    send_sem=send_sem.at[i, step],
                    recv_sem=recv_sem.at[i, step],
                    device_id={"dp": nexts[-way if BACKWARD[i] and step == 0 else way]},
                    device_id_type=MESH,
                )
                hop.start()
                hops[i, step] = hop
    fold_swap.wait()
    small_out[...] = folded[...] + folded_other[...]
    row_swap.wait()
    for copy in list(hops.values()) + list(swaps.values()) + small_hops + small_hands:
        copy.wait_send()


def scatter_all(small, rows, grads, ways, ranks):
    chips, count = ranks // 2, len(grads)
    grads = [g.reshape(ranks, g.shape[0] // ranks, g.shape[1]) for g in grads]
    dma = pltpu.SemaphoreType.DMA
    blocks = [g.shape[1:] for g in grads]
    return pl.pallas_call(
        functools.partial(scatter_kernel, chips, ways),
        out_shape=[jax.ShapeDtypeStruct(v.shape, v.dtype) for v in (small, rows)]
        + [jax.ShapeDtypeStruct(b, jnp.float32) for b in blocks],
        in_specs=[pl.BlockSpec(memory_space=pltpu.VMEM)] * 2
        + [pl.BlockSpec(memory_space=pl.ANY)] * count,
        out_specs=[pl.BlockSpec(memory_space=pltpu.VMEM)] * (count + 2),
        scratch_shapes=[pltpu.VMEM((chips,) + b, jnp.bfloat16) for b in blocks]
        + [pltpu.VMEM((chips,) + b, jnp.bfloat16) for b in blocks]
        + [pltpu.VMEM((chips - 1,) + b, jnp.bfloat16) for b in blocks]
        + [pltpu.VMEM((ranks,) + small.shape, small.dtype)]
        + [pltpu.VMEM(small.shape, small.dtype)] * 2
        + [
            dma((count, chips)),
            dma((count, chips - 1)),
            dma((count, chips - 1)),
            dma((count, chips)),
            dma((count, chips)),
            dma,
            dma((2,)),
            dma((2,)),
            dma((chips - 1,)),
            dma((chips - 1,)),
            dma((chips,)),
            dma((chips,)),
        ],
        compiler_params=pltpu.CompilerParams(
            collective_id=2, has_side_effects=True, vmem_limit_bytes=56 * 1024 * 1024
        ),
    )(small, rows, *grads)


def both(values):
    other = lax.ppermute(values, "tensor", [(0, 1), (1, 0)])
    return jnp.concatenate([values, other], axis=0)


def halves_sum(terms):
    half = terms.shape[0] // 2
    sent = lax.ppermute(terms[half:].astype(jnp.bfloat16), "tensor", [(0, 1), (1, 0)])
    return terms[:half] + sent.astype(jnp.float32)


def reset_masks(segment):
    padded = jnp.concatenate([jnp.full((2,), -1, segment.dtype), segment])
    same_one, same_two = segment == padded[1:-1], segment == padded[:-2]
    masks = jnp.stack([same_one, same_two]).astype(jnp.float32)
    half = segment.shape[0] // 2
    turned = jnp.concatenate([masks[:, half:], masks[:, :half]], axis=1)
    masks = jnp.where(lax.axis_index("tensor") == 0, masks, turned)
    return (masks[0][:, None], masks[1][:, None])


def turn(values, offset):
    return jnp.concatenate([values[-offset:], values[:-offset]], axis=0)


def dot(left, right, dims):
    return lax.dot_general(left, right, (dims, ((), ())), preferred_element_type=jnp.float32)


def local(
    tokens,
    segment_ids,
    norm1_gain,
    in_proj,
    conv_weight,
    out_proj,
    norm2_gain,
    gate_up,
    down_proj,
    cotangent,
    *,
    ranks,
):
    rows, _, channels = in_proj.shape
    inputs = tokens.astype(jnp.float32)
    normed_one, factor_one = rms_forward(inputs, norm1_gain)
    normed_one = normed_one.astype(jnp.bfloat16)
    (normed_other, cot_other), (in_full, out_full, gate_full, up_full, down_full) = gather_all(
        [normed_one, cotangent],
        [
            in_proj.reshape(rows, 3 * channels),
            out_proj,
            gate_up[:, 0, :],
            gate_up[:, 1, :],
            down_proj,
        ],
        WAYS,
        ranks,
    )
    rows_one = jnp.concatenate([normed_one, normed_other], axis=0)
    cot_rows = jnp.concatenate([cotangent, cot_other], axis=0)
    offset = lax.axis_index("tensor") * channels
    kernel = lax.dynamic_slice_in_dim(conv_weight, offset, channels, 1)
    mask_one, mask_two = reset_masks(segment_ids[0])
    projected = dot(rows_one, in_full, ((1,), (0,)))
    b_part = projected[:, :channels]
    c_part = projected[:, channels : 2 * channels]
    x_part = projected[:, 2 * channels :]
    mixed_in = b_part * x_part
    mixed_one = mask_one * turn(mixed_in, 1)
    mixed_two = mask_two * turn(mixed_in, 2)
    conv_out = kernel[0] * mixed_in + kernel[1] * mixed_one + kernel[2] * mixed_two
    gated = (c_part * conv_out).astype(jnp.bfloat16)
    resid = inputs + halves_sum(dot(gated, out_full, ((1,), (1,))))
    normed_two, factor_two = rms_forward(resid, norm2_gain)
    rows_two = both(normed_two.astype(jnp.bfloat16))
    gate_lin = dot(rows_two, gate_full, ((1,), (0,)))
    up_lin = dot(rows_two, up_full, ((1,), (0,)))
    sigmoid_gate = jax.nn.sigmoid(gate_lin)
    activ = gate_lin * sigmoid_gate
    hidden = (activ * up_lin).astype(jnp.bfloat16)
    ffn_terms = dot(hidden, down_full, ((1,), (1,)))
    grad_down = dot(cot_rows, hidden, ((0,), (0,))).astype(jnp.bfloat16)
    back_hidden = dot(cot_rows, down_full, ((1,), (0,)))
    back_gate = (
        back_hidden * up_lin * sigmoid_gate * (1.0 + gate_lin * (1.0 - sigmoid_gate))
    ).astype(jnp.bfloat16)
    back_up = (back_hidden * activ).astype(jnp.bfloat16)
    grad_gate = dot(rows_two, back_gate, ((0,), (0,))).astype(jnp.bfloat16)
    grad_up = dot(rows_two, back_up, ((0,), (0,))).astype(jnp.bfloat16)
    back_normed2 = halves_sum(
        dot(back_gate, gate_full, ((1,), (1,))) + dot(back_up, up_full, ((1,), (1,)))
    )
    resid_part, gain_two = rms_backward(resid, factor_two, norm2_gain, back_normed2)
    back_resid = cotangent.astype(jnp.float32) + resid_part
    resid_rows = both(back_resid.astype(jnp.bfloat16))
    grad_out = dot(resid_rows, gated, ((0,), (0,))).astype(jnp.bfloat16)
    back_gated = dot(resid_rows, out_full, ((1,), (0,)))
    back_c = back_gated * conv_out
    back_conv = back_gated * c_part
    back_mixed = (
        kernel[0] * back_conv
        + turn(kernel[1] * mask_one * back_conv, -1)
        + turn(kernel[2] * mask_two * back_conv, -2)
    )
    conv_local = jnp.stack(
        [
            jnp.sum(back_conv * mixed_in, axis=0),
            jnp.sum(back_conv * mixed_one, axis=0),
            jnp.sum(back_conv * mixed_two, axis=0),
        ]
    )
    back_proj = jnp.concatenate(
        [back_mixed * x_part, back_c, back_mixed * b_part], axis=1
    ).astype(jnp.bfloat16)
    grad_in = dot(rows_one, back_proj, ((0,), (0,))).astype(jnp.bfloat16)
    back_normed1 = halves_sum(dot(back_proj, in_full, ((1,), (1,))))
    input_part, gain_one = rms_backward(inputs, factor_one, norm1_gain, back_normed1)
    grad_tokens = back_resid + input_part
    conv_placed = lax.dynamic_update_slice_in_dim(
        jnp.zeros(conv_weight.shape, jnp.float32), conv_local, offset, 1
    )
    small = jnp.concatenate(
        [gain_one[None], gain_two[None], conv_placed, jnp.zeros_like(conv_placed)], axis=0
    )
    half = ffn_terms.shape[0] // 2
    small, ffn_other, in_shard, out_shard, gate_shard, up_shard, down_shard = scatter_all(
        small,
        ffn_terms[half:].astype(jnp.bfloat16),
        [grad_in, grad_out, grad_gate, grad_up, grad_down],
        WAYS,
        ranks,
    )
    block_out = resid + (ffn_terms[:half] + ffn_other.astype(jnp.float32))
    return (
        block_out,
        grad_tokens,
        small[0],
        in_shard.reshape(in_proj.shape),
        small[2:5],
        out_shard,
        small[1],
        jnp.stack([gate_shard, up_shard], axis=1),
        down_shard,
    )


def solution(mesh):
    placed = (
        P(("dp", "tensor"), None),
        P("dp", None),
        P(),
        P("dp", None, "tensor"),
        P(),
        P("dp", "tensor"),
        P(),
        P("dp", None, "tensor"),
        P("dp", "tensor"),
        P(("dp", "tensor"), None),
    )
    return jax.shard_map(
        functools.partial(local, ranks=mesh.shape["dp"]),
        mesh=mesh,
        in_specs=placed,
        out_specs=(
            P(("dp", "tensor"), None),
            P(("dp", "tensor"), None),
            P(),
            P("dp", None, "tensor"),
            P(),
            P("dp", "tensor"),
            P(),
            P("dp", None, "tensor"),
            P("dp", "tensor"),
        ),
        check_vma=False,
    )
```
